32 devices in a mesh: dp: 4 (over z), fsdp: 8 (over y, x, core).
Axes of the slice: x: 2, y: 2, z: 4, core: 2. Of those that a mesh axis runs over, the one named last changes fastest.
Arguments:
- tokens: bfloat16 [32768, 768], P(('dp', 'fsdp')), may hold values from -6 to 6
- cotangent: bfloat16 [32768, 768], P(('dp', 'fsdp')), may hold values from -6 to 6
- bucket: int32 [64], P(('dp', 'fsdp')), may hold values from 0 to 2, as said below
- lengths: int32 [64, 4], P(('dp', 'fsdp')), may hold values from 0 to 512, as said below
- w_query: bfloat16 [768, 768], P('fsdp'), may hold values from -0.3125 to 0.3125
- b_query: bfloat16 [768], P('fsdp'), may hold values from -2 to 2
- w_key: bfloat16 [768, 768], P('fsdp'), may hold values from -0.3125 to 0.3125
- w_value: bfloat16 [768, 768], P('fsdp'), may hold values from -0.21875 to 0.21875
- b_value: bfloat16 [768], P('fsdp'), may hold values from -2 to 2
- w_out: bfloat16 [768, 768], P('fsdp'), may hold values from -1.25 to 1.25
- b_out: bfloat16 [768], P('fsdp'), may hold values from -2 to 2
- gain_one: bfloat16 [768], P('fsdp'), may hold values from 0.5 to 1.5
- shift_one: bfloat16 [768], P('fsdp'), may hold values from -2 to 2
- w_up: bfloat16 [768, 3072], P('fsdp'), may hold values from -0.21875 to 0.21875
- b_up: bfloat16 [3072], P('fsdp'), may hold values from -2 to 2
- w_down: bfloat16 [3072, 768], P('fsdp'), may hold values from -0.109375 to 0.109375
- b_down: bfloat16 [768], P('fsdp'), may hold values from -2 to 2
- gain_two: bfloat16 [768], P('fsdp'), may hold values from 0.5 to 1.5
- shift_two: bfloat16 [768], P('fsdp'), may hold values from -2 to 2
Outputs:
- output: bfloat16 [32768, 768], P(('dp', 'fsdp'))
- grad_tokens: float32 [32768, 768], P(('dp', 'fsdp'))
- grad_w_query: float32 [768, 768], P('fsdp')
- grad_b_query: float32 [768], P('fsdp')
- grad_w_key: float32 [768, 768], P('fsdp')
- grad_w_value: float32 [768, 768], P('fsdp')
- grad_b_value: float32 [768], P('fsdp')
- grad_w_out: float32 [768, 768], P('fsdp')
- grad_b_out: float32 [768], P('fsdp')
- grad_gain_one: float32 [768], P('fsdp')
- grad_shift_one: float32 [768], P('fsdp')
- grad_w_up: float32 [768, 3072], P('fsdp')
- grad_b_up: float32 [3072], P('fsdp')
- grad_w_down: float32 [3072, 768], P('fsdp')
- grad_b_down: float32 [768], P('fsdp')
- grad_gain_two: float32 [768], P('fsdp')
- grad_shift_two: float32 [768], P('fsdp')
The draws below stay inside these ranges and needn't reach their ends.
Inputs may be any that keep to these rules, and one draw needn't show every extreme that they name: bucket b gives micro-batch segments of 512 >> (2 - b) tokens; bucket[0] is 2. For a micro-batch of bucket b, entries 0 to (1 << (2 - b)) - 1 are its sequences' lengths, each from a quarter of its segment to the whole segment; the other entries are 0; lengths[0, 0] is 512.
All inputs are finite; a program needn't handle non-finite values.
Results may differ from the reference program's by a relative error of at most 0.02.
Values may be sent and summed in bfloat16 or wider, within the bound.
No kernel may reach another device: no remote copies, remote signals or barrier semaphores. Data moves between devices by JAX's collectives and lax.ppermute only.
A program may use at most 192 MiB of HBM per device.

```python
import jax
import jax.numpy as jnp
from jax import lax

D = 768
H = 12
HD = 64
FF = 3072
SLOT = 512
MICROS = 64
TOKENS = 32768


def draw_common(key):
    key_bucket, key_length = jax.random.split(jax.random.fold_in(key, 17))
    bucket = jax.random.randint(key_bucket, (MICROS,), 0, 3).astype(jnp.int32)
    bucket = bucket.at[0].set(2)
    seg_len = jnp.right_shift(jnp.int32(SLOT), 2 - bucket)
    seg_count = jnp.left_shift(jnp.int32(1), 2 - bucket)
    raw_bits = jax.random.randint(key_length, (MICROS, 4), 0, 1 << 20).astype(jnp.int32)
    lowest = seg_len // 4
    seq_lens = lowest[:, None] + raw_bits % (seg_len - lowest + 1)[:, None]
    slot_ids = jnp.arange(4, dtype=jnp.int32)[None, :]
    seq_lens = jnp.where(slot_ids < seg_count[:, None], seq_lens, 0)
    seq_lens = seq_lens.at[0, 0].set(SLOT)
    return (bucket, seq_lens.astype(jnp.int32))


def draw_bucket(key, part):
    return draw_common(key)[0]


def draw_lengths(key, part):
    return draw_common(key)[1]


def steps_of(stream_key, shape, cuts, least, largest):
    factor_of, own = 1.0, jax.random.fold_in(stream_key, 6)
    for axis_at, parts in cuts:
        steps = jnp.exp(jax.random.uniform(jax.random.fold_in(own, axis_at), (parts,), jnp.float32, least / len(cuts), largest / len(cuts)))
        factor_of = factor_of * jnp.repeat(steps, shape[axis_at] // parts).reshape([-1 if axis == axis_at else 1 for axis in range(len(shape))])
    return factor_of


def gaussian(own_key, shape, scale, limit, cuts=(), held_as=jnp.bfloat16):
    result = jax.random.normal(own_key, shape, jnp.float32) * scale
    if len(cuts) > 0:
        result = steps_of(own_key, shape, cuts, -0.22, 0.18) * result
    return jnp.clip(result, min=-limit, max=limit).astype(held_as)


def setup_inputs(seed: int = 0) -> dict:
    streams_of = jax.random.split(jax.random.key(seed), 20)
    tokens = gaussian(streams_of[0], (TOKENS, D), 1.0, 6.0, ((0, 32),))
    cotangent = gaussian(streams_of[1], (TOKENS, D), 1.0, 6.0, ((0, 32),))
    bucket = draw_bucket(jax.random.fold_in(streams_of[19], 71), 0)
    lengths = draw_lengths(jax.random.fold_in(streams_of[19], 71), 0)
    w_query = gaussian(streams_of[4], (D, D), (D // 2) ** -0.5, 0.3125, ((0, 8),))
    b_query = gaussian(streams_of[5], (D,), 0.3, 2.0, ((0, 8),))
    w_key = gaussian(streams_of[6], (D, D), (D // 2) ** -0.5, 0.3125, ((0, 8),))
    w_value = gaussian(streams_of[7], (D, D), D ** -0.5, 0.21875, ((0, 8),))
    b_value = gaussian(streams_of[8], (D,), 0.3, 2.0, ((0, 8),))
    w_out = gaussian(streams_of[9], (D, D), (D // 32) ** -0.5, 1.25, ((0, 8),))
    b_out = gaussian(streams_of[10], (D,), 0.3, 2.0, ((0, 8),))
    gain_one = jnp.clip(1.0 + 0.1 * jax.random.normal(streams_of[11], (D,), jnp.float32), 0.5, 1.5).astype(jnp.bfloat16)
    shift_one = gaussian(streams_of[12], (D,), 0.3, 2.0, ((0, 8),))
    w_up = gaussian(streams_of[13], (D, FF), D ** -0.5, 0.21875, ((0, 8),))
    b_up = gaussian(streams_of[14], (FF,), 0.3, 2.0, ((0, 8),))
    w_down = gaussian(streams_of[15], (FF, D), FF ** -0.5, 0.109375, ((0, 8),))
    b_down = gaussian(streams_of[16], (D,), 0.3, 2.0, ((0, 8),))
    gain_two = jnp.clip(1.0 + 0.1 * jax.random.normal(streams_of[17], (D,), jnp.float32), 0.5, 1.5).astype(jnp.bfloat16)
    shift_two = gaussian(streams_of[18], (D,), 0.3, 2.0, ((0, 8),))
    return dict(tokens=tokens, cotangent=cotangent, bucket=bucket, lengths=lengths, w_query=w_query, b_query=b_query, w_key=w_key, w_value=w_value, b_value=b_value, w_out=w_out, b_out=b_out, gain_one=gain_one, shift_one=shift_one, w_up=w_up, b_up=b_up, w_down=w_down, b_down=b_down, gain_two=gain_two, shift_two=shift_two)


HIGHEST = lax.Precision.HIGHEST
MASKED = -1000000000.0
EPSILON = 1e-05

@jax.custom_vjp
def low(v):
    return lax.optimization_barrier(v.astype(jnp.bfloat16)).astype(jnp.float32)

@jax.custom_vjp
def low_back(v):
    return v

def low_keep(v):
    return (low(v), None)

def low_pass(kept, grad):
    return (grad,)

def back_keep(v):
    return (v, None)

def back_low(kept, grad):
    return (low(grad),)
low.defvjp(low_keep, low_pass)
low_back.defvjp(back_keep, back_low)

def key_mask(bucket_id, seq_lens, slot_count):
    seg_len = jnp.right_shift(jnp.int32(slot_count), (2 - bucket_id).astype(jnp.int32))
    where_at = jnp.arange(slot_count, dtype=jnp.int32)
    seg_id = where_at // seg_len
    inside = where_at - seg_id * seg_len
    choose = seg_id[:, None] == jnp.arange(4, dtype=jnp.int32)[None, :]
    limits = lax.optimization_barrier(jnp.sum(jnp.where(choose, seq_lens[None, :], 0), axis=1))
    live_rows = inside < limits
    allowed = (seg_id[:, None] == seg_id[None, :]) & live_rows[None, :]
    return (allowed, live_rows)

def layer_norm(row_data, gain_vec, shift_vec):
    row_mean = lax.optimization_barrier(jnp.mean(row_data, axis=-1, keepdims=True))
    centered = row_data - row_mean
    variance = lax.optimization_barrier(jnp.mean(centered * centered, axis=-1, keepdims=True))
    return centered * lax.rsqrt(variance + EPSILON) * gain_vec + shift_vec

def encoder_layer(row_data, params, allowed):
    w_query, b_query, w_key, w_value, b_value, w_out, b_out, gain_one, shift_one, w_up, b_up, w_down, b_down, gain_two, shift_two = params
    slot_count = row_data.shape[0]

    def project(inputs_low, matrix, offset):
        return jnp.dot(inputs_low, matrix, precision=HIGHEST) + offset
    query_low = low(low_back(project(row_data, w_query, b_query))).reshape(slot_count, H, HD)
    key_low = low(low_back(jnp.dot(row_data, w_key, precision=HIGHEST))).reshape(slot_count, H, HD)
    value_low = low(low_back(project(row_data, w_value, b_value))).reshape(slot_count, H, HD)
    scores = low_back(jnp.einsum('qhd,khd->hqk', query_low, key_low, precision=HIGHEST) * 0.125)
    scores = jnp.where(allowed[None], scores, MASKED)
    attn_probs = low(jax.nn.softmax(scores, axis=-1))
    context = jnp.einsum('hqk,khd->qhd', attn_probs, value_low, precision=HIGHEST).reshape(slot_count, D)
    context = low(low_back(context))
    attended = low_back(project(context, w_out, b_out))
    hidden = layer_norm(row_data + attended, gain_one, shift_one)
    upward = low_back(project(low(hidden), w_up, b_up))
    active = low(jax.nn.gelu(upward, approximate=False))
    downward = low_back(project(active, w_down, b_down))
    return layer_norm(hidden + downward, gain_two, shift_two)

def reference(tokens, cotangent, bucket, lengths, w_query, b_query, w_key, w_value, b_value, w_out, b_out, gain_one, shift_one, w_up, b_up, w_down, b_down, gain_two, shift_two):
    weights = tuple((item.astype(jnp.float32) for item in (w_query, b_query, w_key, w_value, b_value, w_out, b_out, gain_one, shift_one, w_up, b_up, w_down, b_down, gain_two, shift_two)))
    tok_all = tokens.astype(jnp.float32).reshape(MICROS, SLOT, D)
    cot_all = cotangent.astype(jnp.float32).reshape(MICROS, SLOT, D)

    def one_micro(running, batch_item):
        tok_rows, cot_rows, bucket_id, seq_lens = batch_item
        allowed, live_rows = key_mask(bucket_id, seq_lens, SLOT)
        output, pull = jax.vjp(lambda row_data, *params: encoder_layer(row_data, params, allowed), tok_rows, *weights)
        gradients = pull(cot_rows * live_rows[:, None].astype(cot_rows.dtype))
        running = tuple((acc + new_part for acc, new_part in zip(running, gradients[1:])))
        return (running, (output.astype(jnp.bfloat16), gradients[0]))
    zero_sums = tuple((jnp.zeros_like(item) for item in weights))
    totals, (outputs, token_grads) = lax.scan(one_micro, zero_sums, (tok_all, cot_all, bucket, lengths))
    return (outputs.reshape(TOKENS, D), token_grads.reshape(TOKENS, D), totals[0], totals[1], totals[2], totals[3], totals[4], totals[5], totals[6], totals[7], totals[8], totals[9], totals[10], totals[11], totals[12], totals[13], totals[14])
```

```python
import functools

import jax
import jax.numpy as jnp
from jax import lax
from jax.sharding import PartitionSpec as P

D = 768
H = 12
HD = 64


MASKED = -1000000000.0
EPSILON = 1e-05


def for_sending(x):
    return jax.tree.map(lambda a: a.astype(jnp.bfloat16) if a.dtype == jnp.float32 else a, x)


def key_mask(bucket_id, seq_lens, slot_count):
    seg_len = jnp.right_shift(jnp.int32(slot_count), 2 - bucket_id)
    where_at = jnp.arange(slot_count, dtype=jnp.int32)
    seg_id = where_at // seg_len
    inside = where_at - seg_id * seg_len
    choose = seg_id[:, None] == jnp.arange(4, dtype=jnp.int32)[None, :]
    limits = jnp.sum(jnp.where(choose, seq_lens[None, :], 0), axis=1)
    live_rows = inside < limits
    allowed = (seg_id[:, None] == seg_id[None, :]) & live_rows[None, :]
    return (allowed, live_rows)


def layer_norm(row_data, gain_vec, shift_vec):
    row_mean = jnp.mean(row_data, axis=-1, keepdims=True)
    centered = row_data - row_mean
    variance = jnp.mean(centered * centered, axis=-1, keepdims=True)
    return centered * lax.rsqrt(variance + EPSILON) * gain_vec + shift_vec


def gelu_exact(inputs_pre):
    return jax.nn.gelu(inputs_pre, approximate=False)


def project(inputs_low, matrix, offset):
    return jnp.dot(inputs_low, matrix, preferred_element_type=jnp.float32) + offset.astype(
        jnp.float32
    )


def head_scores(query_low, key_low, allowed):
    scores = (
        jnp.einsum("qhd,khd->hqk", query_low, key_low, preferred_element_type=jnp.float32) * 0.125
    )
    return jnp.where(allowed[None], scores, MASKED)


def forward(weights, tok_rows, allowed):
    (
        w_query,
        b_query,
        w_key,
        w_value,
        b_value,
        w_out,
        b_out,
        gain_one,
        shift_one,
        w_up,
        b_up,
        w_down,
        b_down,
        gain_two,
        shift_two,
    ) = weights
    slot_count = tok_rows.shape[0]
    query_low = project(tok_rows, w_query, b_query).astype(jnp.bfloat16).reshape(slot_count, H, HD)
    key_low = (
        jnp.dot(tok_rows, w_key, preferred_element_type=jnp.float32)
        .astype(jnp.bfloat16)
        .reshape(slot_count, H, HD)
    )
    value_low = project(tok_rows, w_value, b_value).astype(jnp.bfloat16).reshape(slot_count, H, HD)
    scores = head_scores(query_low, key_low, allowed)
    row_max = jnp.max(scores, axis=-1, keepdims=True)
    exp_scores = jnp.exp(scores - row_max)
    row_total = jnp.sum(exp_scores, axis=-1, keepdims=True)
    attn_probs = exp_scores / row_total
    log_total = row_max + jnp.log(row_total)
    context = (
        jnp.einsum(
            "hqk,khd->qhd",
            attn_probs.astype(jnp.bfloat16),
            value_low,
            preferred_element_type=jnp.float32,
        )
        .reshape(slot_count, D)
        .astype(jnp.bfloat16)
    )
    resid_one = tok_rows.astype(jnp.float32) + project(context, w_out, b_out)
    hidden, norm_one = jax.vjp(
        layer_norm, resid_one, gain_one.astype(jnp.float32), shift_one.astype(jnp.float32)
    )
    hidden_low = hidden.astype(jnp.bfloat16)
    upward = project(hidden_low, w_up, b_up)
    active, gelu_back = jax.vjp(gelu_exact, upward)
    active_low = active.astype(jnp.bfloat16)
    resid_two = hidden + project(active_low, w_down, b_down)
    output, norm_two = jax.vjp(
        layer_norm, resid_two, gain_two.astype(jnp.float32), shift_two.astype(jnp.float32)
    )
    kept = (
        query_low,
        key_low,
        value_low,
        log_total,
        context,
        norm_one,
        hidden_low,
        gelu_back,
        active_low,
        norm_two,
    )
    return (output.astype(jnp.bfloat16), kept)


def backward(weights, tok_rows, allowed, live_rows, cot_rows, kept):
    (
        w_query,
        b_query,
        w_key,
        w_value,
        b_value,
        w_out,
        b_out,
        gain_one,
        shift_one,
        w_up,
        b_up,
        w_down,
        b_down,
        gain_two,
        shift_two,
    ) = weights
    (
        query_low,
        key_low,
        value_low,
        log_total,
        context,
        norm_one,
        hidden_low,
        gelu_back,
        active_low,
        norm_two,
    ) = kept
    slot_count = tok_rows.shape[0]
    grad_rows = cot_rows.astype(jnp.float32) * live_rows[:, None].astype(jnp.float32)
    d_resid_two, g_gain_two, g_shift_two = norm_two(grad_rows)
    d_down = d_resid_two.astype(jnp.bfloat16)
    g_b_down = jnp.sum(d_down.astype(jnp.float32), axis=0)
    g_w_down = jnp.einsum("tf,td->fd", active_low, d_down, preferred_element_type=jnp.float32)
    d_active = jnp.einsum("td,fd->tf", d_down, w_down, preferred_element_type=jnp.float32)
    (d_upward,) = gelu_back(d_active)
    d_up_low = d_upward.astype(jnp.bfloat16)
    g_b_up = jnp.sum(d_up_low.astype(jnp.float32), axis=0)
    g_w_up = jnp.einsum("td,tf->df", hidden_low, d_up_low, preferred_element_type=jnp.float32)
    d_hidden = d_resid_two + jnp.einsum(
        "tf,df->td", d_up_low, w_up, preferred_element_type=jnp.float32
    )
    d_resid_one, g_gain_one, g_shift_one = norm_one(d_hidden)
    d_attended = d_resid_one.astype(jnp.bfloat16)
    g_b_out = jnp.sum(d_attended.astype(jnp.float32), axis=0)
    g_w_out = jnp.einsum("td,te->de", context, d_attended, preferred_element_type=jnp.float32)
    d_context = (
        jnp.einsum("te,de->td", d_attended, w_out, preferred_element_type=jnp.float32)
        .astype(jnp.bfloat16)
        .reshape(slot_count, H, HD)
    )
    attn_probs = jnp.exp(head_scores(query_low, key_low, allowed) - log_total)
    d_values = (
        jnp.einsum(
            "hqk,qhd->khd",
            attn_probs.astype(jnp.bfloat16),
            d_context,
            preferred_element_type=jnp.float32,
        )
        .reshape(slot_count, D)
        .astype(jnp.bfloat16)
    )
    d_probs = jnp.einsum("qhd,khd->hqk", d_context, value_low, preferred_element_type=jnp.float32)
    d_scores = (
        attn_probs * (d_probs - jnp.sum(attn_probs * d_probs, axis=-1, keepdims=True))
    ).astype(jnp.bfloat16)
    d_query = (
        (jnp.einsum("hqk,khd->qhd", d_scores, key_low, preferred_element_type=jnp.float32) * 0.125)
        .reshape(slot_count, D)
        .astype(jnp.bfloat16)
    )
    d_keys = (
        (
            jnp.einsum("hqk,qhd->khd", d_scores, query_low, preferred_element_type=jnp.float32)
            * 0.125
        )
        .reshape(slot_count, D)
        .astype(jnp.bfloat16)
    )
    g_b_query = jnp.sum(d_query.astype(jnp.float32), axis=0)
    g_b_value = jnp.sum(d_values.astype(jnp.float32), axis=0)
    g_w_query = jnp.einsum("td,te->de", tok_rows, d_query, preferred_element_type=jnp.float32)
    g_w_key = jnp.einsum("td,te->de", tok_rows, d_keys, preferred_element_type=jnp.float32)
    g_w_value = jnp.einsum("td,te->de", tok_rows, d_values, preferred_element_type=jnp.float32)
    d_tokens = (
        d_resid_one
        + jnp.einsum("te,de->td", d_query, w_query, preferred_element_type=jnp.float32)
        + jnp.einsum("te,de->td", d_keys, w_key, preferred_element_type=jnp.float32)
        + jnp.einsum("te,de->td", d_values, w_value, preferred_element_type=jnp.float32)
    )
    gradients = (
        g_w_query,
        g_b_query,
        g_w_key,
        g_w_value,
        g_b_value,
        g_w_out,
        g_b_out,
        g_gain_one,
        g_shift_one,
        g_w_up,
        g_b_up,
        g_w_down,
        g_b_down,
        g_gain_two,
        g_shift_two,
    )
    return (d_tokens, gradients)


def bits_of(count):
    bits = [1 << i for i in range(count.bit_length() - 1)]
    assert count == 1 << len(bits), "axis size"
    return bits


def swap(x, bit, axis, count):
    return lax.ppermute(x, axis, [(i, i ^ bit) for i in range(count)])


def gather_rel(x, order, count):
    pieces = {0: x}
    for bit in order:
        pieces.update({m | bit: swap(p, bit, "fsdp", count) for m, p in list(pieces.items())})
    return pieces


def place(pieces, me):
    rows = pieces[0].shape[0]
    whole = jnp.zeros((rows * len(pieces), pieces[0].shape[1]), pieces[0].dtype)
    for m, piece in pieces.items():
        whole = lax.dynamic_update_slice_in_dim(whole, piece, (me ^ m) * rows, axis=0)
    return whole


def add_low(a, b):
    return (a.astype(jnp.float32) + b.astype(jnp.float32)).astype(jnp.bfloat16)


def reduce_rel(parts, order, count):
    for bit in order:
        sent = [m for m in sorted(parts) if m & bit]
        got = swap(jnp.concatenate([parts[m] for m in sent], axis=0), bit, "fsdp", count)
        got = jnp.split(got, len(sent), axis=0)
        parts = {m ^ bit: add_low(parts[m ^ bit], g) for m, g in zip(sent, got)}
    return parts[0]


def sum_over_dp(x, count):
    at = lax.axis_index("dp")
    bits = bits_of(count)
    for bit in bits:
        low, high = jnp.split(x, 2, axis=0)
        upper = (at & bit) != 0
        got = swap(jnp.where(upper, low, high), bit, "dp", count)
        x = add_low(jnp.where(upper, high, low), got)
    for bit in reversed(bits):
        upper = (at & bit) != 0
        got = swap(x, bit, "dp", count)
        x = jnp.concatenate([jnp.where(upper, got, x), jnp.where(upper, x, got)], axis=0)
    return x


VECTORS = (1, 4, 6, 7, 8, 10, 12, 13, 14)


def pack_vectors(vecs, shard):
    return jnp.concatenate([v.reshape(-1, shard) for v in vecs], axis=0)


def on_device(sizes, tokens, cotangent, bucket, lengths, *shards):
    dp, fsdp = sizes
    me = lax.axis_index("fsdp")
    chip_bits = bits_of(fsdp)[1:]
    up, down = chip_bits + [1], chip_bits[::-1] + [1]
    model = tokens.shape[1]
    shard = shards[0].shape[0]
    micro_count = bucket.shape[0]
    slot_count = tokens.shape[0] // micro_count

    vecs = pack_vectors([shards[i] for i in VECTORS], shard)
    half = shard // 2
    first = jnp.concatenate([shards[0], shards[2][:half]], axis=0)
    second = jnp.concatenate([shards[3], shards[2][half:]], axis=0)
    got_v = gather_rel(vecs, down, fsdp)
    got_1, got_2 = gather_rel(first, up, fsdp), gather_rel(second, down, fsdp)
    got_o1, got_o2 = gather_rel(shards[5][:half], up, fsdp), gather_rel(shards[5][half:], down, fsdp)
    got_up, got_down = gather_rel(shards[9], up, fsdp), gather_rel(shards[11], down, fsdp)

    weights = [None] * 15
    weights[0] = place({m: p[:shard] for m, p in got_1.items()}, me)
    weights[3] = place({m: p[:shard] for m, p in got_2.items()}, me)
    weights[2] = place(
        {m: jnp.concatenate([p[shard:], got_2[m][shard:]], axis=0) for m, p in got_1.items()}, me
    )
    weights[5] = place(
        {m: jnp.concatenate([p, got_o2[m]], axis=0) for m, p in got_o1.items()}, me
    )
    weights[9] = place(got_up, me)
    weights[11] = place(got_down, me)
    rows = vecs.shape[0]
    all_vecs = place(got_v, me).reshape(fsdp, rows, shard)
    at = 0
    for i in VECTORS:
        n = shards[i].shape[0] // shard
        weights[i] = all_vecs[:, at : at + n].reshape(-1)
        at += n
    weights = tuple(weights)

    summed = None
    outputs = []
    token_grads = []
    for i in range(micro_count):
        tok_rows = lax.slice_in_dim(tokens, i * slot_count, (i + 1) * slot_count, axis=0)
        cot_rows = lax.slice_in_dim(cotangent, i * slot_count, (i + 1) * slot_count, axis=0)
        allowed, live_rows = key_mask(bucket[i], lengths[i], slot_count)
        output, kept = forward(weights, tok_rows, allowed)
        outputs.append(output)
        d_tokens, gradients = backward(weights, tok_rows, allowed, live_rows, cot_rows, kept)
        token_grads.append(d_tokens)
        summed = gradients if summed is None else jax.tree.map(jnp.add, summed, gradients)

    def relative(whole):
        n = whole.shape[0] // fsdp
        return {
            m: lax.dynamic_slice_in_dim(whole, (me ^ m) * n, n, axis=0).astype(jnp.bfloat16)
            for m in range(fsdp)
        }

    core_first_up, core_first_down = [1] + chip_bits, [1] + chip_bits[::-1]

    def reduced(whole, order):
        return sum_over_dp(reduce_rel(relative(whole), order, fsdp), dp).astype(jnp.float32)

    finals = [None] * 15
    finals[11] = reduced(summed[11], core_first_down)
    finals[9] = reduced(summed[9], core_first_up)
    finals[5] = reduced(summed[5], core_first_up)
    for i, order in ((0, core_first_up), (2, core_first_down), (3, core_first_up)):
        finals[i] = reduced(summed[i], order)
    by_shard = jnp.concatenate(
        [summed[i].reshape(fsdp, -1, shard) for i in VECTORS], axis=1
    )
    pad = (-rows) % (2 * dp)
    by_shard = jnp.pad(by_shard, ((0, 0), (0, pad), (0, 0)))
    small = reduced(by_shard.reshape(fsdp * (rows + pad), shard), core_first_down)
    at = 0
    for i in VECTORS:
        n = shards[i].shape[0] // shard
        finals[i] = small[at : at + n].reshape(-1)
        at += n
    return (jnp.concatenate(outputs, axis=0), jnp.concatenate(token_grads, axis=0)) + tuple(finals)


def solution(mesh):
    placed = (
        P(("dp", "fsdp"), None),
        P(("dp", "fsdp"), None),
        P(("dp", "fsdp")),
        P(("dp", "fsdp"), None),
        P("fsdp", None),
        P("fsdp"),
        P("fsdp", None),
        P("fsdp", None),
        P("fsdp"),
        P("fsdp", None),
        P("fsdp"),
        P("fsdp"),
        P("fsdp"),
        P("fsdp", None),
        P("fsdp"),
        P("fsdp", None),
        P("fsdp"),
        P("fsdp"),
        P("fsdp"),
    )
    sizes = (mesh.shape["dp"], mesh.shape["fsdp"])
    return jax.shard_map(
        functools.partial(on_device, sizes),
        mesh=mesh,
        in_specs=placed,
        out_specs=(
            P(("dp", "fsdp"), None),
            P(("dp", "fsdp"), None),
            P("fsdp", None),
            P("fsdp"),
            P("fsdp", None),
            P("fsdp", None),
            P("fsdp"),
            P("fsdp", None),
            P("fsdp"),
            P("fsdp"),
            P("fsdp"),
            P("fsdp", None),
            P("fsdp"),
            P("fsdp", None),
            P("fsdp"),
            P("fsdp"),
            P("fsdp"),
        ),
        check_vma=False,
    )
```

```python
import functools

import jax
import jax.numpy as jnp
from jax import lax
from jax.experimental import pallas as pl
from jax.experimental.pallas import tpu as pltpu
from jax.sharding import PartitionSpec as P

HEAD = 64
EPSILON = 1e-05
BLOCKED = -8000000000.0
LOW = jnp.bfloat16
F32 = jnp.float32
ANY = pl.BlockSpec(memory_space=pl.ANY)
NN = (((1,), (0,)), ((), ()))
NT = (((1,), (1,)), ((), ()))
TN = (((0,), (0,)), ((), ()))


def mm(a, b, dims=NN):
    return lax.dot_general(a, b, dims, preferred_element_type=F32)


def shape(dims, dtype=LOW):
    return jax.ShapeDtypeStruct(dims, dtype)


def whole(*dims):
    return pl.BlockSpec(dims, lambda *_: (0,) * len(dims))


def params(grid_rank):
    return pltpu.CompilerParams(
        dimension_semantics=("arbitrary",) * grid_rank, vmem_limit_bytes=60 * 2**20
    )


def cost(flops, nbytes, exps=0):
    return pl.CostEstimate(
        flops=int(flops), bytes_accessed=int(nbytes), transcendentals=int(exps)
    )


def bits_of(count):
    bits = [1 << i for i in range(count.bit_length() - 1)]
    assert count == 1 << len(bits), "axis size"
    return bits


def swap(x, bit, axis, count):
    return lax.ppermute(x, axis, [(i, i ^ bit) for i in range(count)])


def gather_rel(x, order, count):
    pieces = {0: x}
    for bit in order:
        pieces.update({m | bit: swap(p, bit, "fsdp", count) for m, p in list(pieces.items())})
    return [pieces[m] for m in range(count)]


def reorder(stacked, me):
    count = stacked.shape[0]
    bits = bits_of(count)
    x = stacked.reshape((2,) * len(bits) + stacked.shape[1:])
    for i, bit in enumerate(reversed(bits)):
        x = jnp.where((me & bit) != 0, jnp.flip(x, i), x)
    return x.reshape(stacked.shape)


def add_low(a, b):
    return (a.astype(F32) + b.astype(F32)).astype(LOW)


def reduce_chips(parts, order, count):
    for bit in order:
        sent = [m for m in sorted(parts) if m & bit]
        if len(sent) == 1:
            got = [swap(parts[sent[0]], bit, "fsdp", count)]
        else:
            got = swap(jnp.concatenate([parts[m] for m in sent], axis=0), bit, "fsdp", count)
            got = jnp.split(got, len(sent), axis=0)
        parts = {m ^ bit: add_low(parts[m ^ bit], g) for m, g in zip(sent, got)}
    return parts[0]


def sum_over_dp(x, count):
    at = lax.axis_index("dp")
    bits = bits_of(count)
    for bit in bits:
        low, high = jnp.split(x, 2, axis=0)
        upper = (at & bit) != 0
        got = swap(jnp.where(upper, low, high), bit, "dp", count)
        x = add_low(jnp.where(upper, high, low), got)
    for bit in reversed(bits):
        upper = (at & bit) != 0
        got = swap(x, bit, "dp", count)
        x = jnp.concatenate([jnp.where(upper, got, x), jnp.where(upper, x, got)], axis=0)
    return x


def place_rows(pieces, me):
    stacked = reorder(jnp.stack(pieces), me)
    return stacked.reshape((-1,) + pieces[0].shape[1:])


def copy_plan(sources, shard):
    plan = []
    for count, base, row, rows, target, offset in sources:
        for m in range(count):
            plan.append((base + m, row, rows, target, m, offset, shard))
    return plan


def run_copies(plan, me, operands, targets, sems):
    copies = []
    for i, (src, row, rows, target, m, offset, shard) in enumerate(plan):
        at = pl.multiple_of((me ^ m) * shard + offset, 16) if shard else offset
        copies.append(
            pltpu.make_async_copy(
                operands[src].at[pl.ds(row, rows), :],
                targets[target].at[pl.ds(at, rows), :],
                sems.at[i],
            )
        )
    for c in copies:
        c.start()
    return copies


def qkv_kernel(plan, count, info, tok, bias, *refs):
    pieces, (q, k, v, wq, wk, wv), sems = refs[:count], refs[count : count + 6], refs[count + 6]

    @pl.when(pl.program_id(0) == 0)
    def _():
        for c in run_copies(plan, info[0], pieces, (wq, wk, wv), sems):
            c.wait()

    rows = tok[...]
    q[...] = (mm(rows, wq[...]) + bias[0:1, :]).astype(LOW)
    k[...] = mm(rows, wk[...]).astype(LOW)
    v[...] = (mm(rows, wv[...]) + bias[1:2, :]).astype(LOW)


def qkv_call(info, tokens, bias, pieces, plan, tile=256):
    rows, model = tokens.shape
    row_block = pl.BlockSpec((tile, model), lambda i, _: (i, 0))
    return pl.pallas_call(
        functools.partial(qkv_kernel, plan, len(pieces)),
        out_shape=[shape((rows, model))] * 3 + [shape((model, model))] * 3,
        grid_spec=pltpu.PrefetchScalarGridSpec(
            num_scalar_prefetch=1,
            grid=(rows // tile,),
            in_specs=[row_block, whole(2, model)] + [ANY] * len(pieces),
            out_specs=[row_block] * 3 + [whole(model, model)] * 3,
            scratch_shapes=[pltpu.SemaphoreType.DMA((len(plan),))],
        ),
        compiler_params=params(1),
        cost_estimate=cost(6 * rows * model * model, 8 * rows * model + 12 * model * model),
        name="qkv",
    )(info, tokens, bias, *pieces)


def blocked_keys(info, micro, micros, slots):
    shift = slots.bit_length() - 3 + info[1 + micro]
    u = lax.broadcasted_iota(jnp.int32, (slots, 128), 0)
    j = lax.broadcasted_iota(jnp.int32, (slots, 128), 1) & (HEAD - 1)
    base = 1 + micros + 4 * micro
    limit = jnp.where(
        j < 2,
        jnp.where(j == 0, info[base], info[base + 1]),
        jnp.where(j == 2, info[base + 2], info[base + 3]),
    )
    inside = u - (j << shift)
    fine = ((u >> shift) == j) & (inside < limit)
    return jnp.where((j < 4) & jnp.logical_not(fine), BLOCKED, 0.0).astype(LOW)


def segment_rows(info, micro, slots):
    shift = slots.bit_length() - 3 + info[1 + micro]
    j = lax.broadcasted_iota(jnp.int32, (HEAD, slots), 0)
    t = lax.broadcasted_iota(jnp.int32, (HEAD, slots), 1)
    return jnp.where((t >> shift) == j, 1.0, 0.0).astype(LOW)


def attend_kernel(micros, info, q, k, v, context, probs, blocked, segments):
    micro = pl.program_id(0)
    slots = q.shape[0]

    @pl.when(pl.program_id(1) == 0)
    def _():
        blocked[...] = blocked_keys(info, micro, micros, slots)
        segments[...] = segment_rows(info, micro, slots)

    keys = k[...]
    q_t = q[...].T
    v_t = v[...].T
    lane = lax.broadcasted_iota(jnp.int32, keys.shape, 1)
    seg = segments[...]
    block = blocked[...]
    factor = 0.125 * 1.4426950408889634
    parts = []
    for h in range(2):
        mine = (lane < HEAD) if h == 0 else (lane >= HEAD)
        left = jnp.where(mine, keys, block)
        mine_q = q_t[h * HEAD : (h + 1) * HEAD]
        right = jnp.concatenate([mine_q, seg] if h == 0 else [seg, mine_q], axis=0)
        scores = mm(left, right)
        top = jnp.max(scores, axis=0, keepdims=True)
        exps = jnp.exp2(scores * factor - top * factor)
        total = jnp.sum(exps, axis=0, keepdims=True)
        low = (exps * (1.0 / total)).astype(LOW)
        probs[h] = low
        parts.append(mm(v_t[h * HEAD : (h + 1) * HEAD], low))
    context[...] = jnp.concatenate(parts, axis=0).T.astype(LOW)


def attend_call(info, q, k, v, micros):
    rows, model = q.shape
    slots, pairs = rows // micros, model // 128
    pair = pl.BlockSpec((slots, 128), lambda i, j, _: (i, j))
    return pl.pallas_call(
        functools.partial(attend_kernel, micros),
        out_shape=[shape((rows, model)), shape((micros * 2 * pairs, slots, slots))],
        grid_spec=pltpu.PrefetchScalarGridSpec(
            num_scalar_prefetch=1,
            grid=(micros, pairs),
            in_specs=[pair] * 3,
            out_specs=[
                pair,
                pl.BlockSpec((2, slots, slots), lambda i, j, _: (i * pairs + j, 0, 0)),
            ],
            scratch_shapes=[pltpu.VMEM((slots, 128), LOW), pltpu.VMEM((HEAD, slots), LOW)],
        ),
        compiler_params=params(2),
        cost_estimate=cost(
            16 * rows * slots * model,
            8 * rows * model + 4 * rows * slots * pairs,
            2 * rows * slots * pairs,
        ),
        name="attend",
    )(info, q, k, v)


def normal(x):
    mean = jnp.mean(x, axis=-1, keepdims=True)
    centered = x - mean
    variance = jnp.mean(centered * centered, axis=-1, keepdims=True)
    scale = lax.rsqrt(variance + EPSILON)
    return centered * scale, scale


def normal_back(e, n, scale):
    first = jnp.mean(e, axis=-1, keepdims=True)
    second = jnp.mean(e * n, axis=-1, keepdims=True)
    return (e - first - n * second) * scale


def gelu_both(x):
    size = jnp.abs(x)
    t = 1.0 / (1.0 + size * (0.3275911 * 0.7071067811865476))
    e = jnp.exp2(x * x * (-0.5 * 1.4426950408889634))
    series = 0.5 * 1.061405429
    for c in (-1.453152027, 1.421413741, -0.284496736, 0.254829592):
        series = series * t + 0.5 * c
    tail = series * t * e
    phi = jnp.where(x >= 0, 1.0 - tail, tail)
    return x * phi, phi + x * e * 0.3989422804014327


def colsum(x):
    return jnp.sum(x, axis=0, keepdims=True)


def middle_kernel(
    plan, count, micros, slots, info, tok, ctx, cot, vec, b_up, *refs
):
    pieces = refs[:count]
    (out, active, d_up, hid_low, d_down, d_res, d_att, d_ctx, sums, sum_up) = refs[
        count : count + 10
    ]
    wo, wu, wd, slope, sems = refs[count + 10 :]
    step = pl.program_id(0)

    @pl.when(step == 0)
    def _():
        for c in run_copies(plan, info[0], pieces, (wo, wu, wd), sems):
            c.wait()
        sums[...] = jnp.zeros_like(sums)
        sum_up[...] = jnp.zeros_like(sum_up)

    tile, model = tok.shape
    inner = active.shape[1]
    part = 768
    b_out, gain_1, shift_1 = vec[0:1, :], vec[1:2, :], vec[2:3, :]
    b_down, gain_2, shift_2 = vec[3:4, :], vec[4:5, :], vec[5:6, :]
    res_1 = tok[...].astype(F32) + (mm(ctx[...], wo[...]) + b_out)
    n_1, s_1 = normal(res_1)
    hidden = n_1 * gain_1 + shift_1
    low = hidden.astype(LOW)
    hid_low[...] = low
    down = jnp.zeros((tile, model), F32)
    for c in range(0, inner, part):
        x = mm(low, wu[:, c : c + part]) + b_up[:, c : c + part]
        a, g = gelu_both(x)
        a = a.astype(LOW)
        active[:, c : c + part] = a
        slope[:, c : c + part] = g
        down = down + mm(a, wd[c : c + part, :])
    n_2, s_2 = normal(hidden + (down + b_down))
    out[...] = (n_2 * gain_2 + shift_2).astype(LOW)

    per_micro = slots // tile
    micro = step // per_micro
    shift = slots.bit_length() - 3 + info[1 + micro]
    t = lax.broadcasted_iota(jnp.int32, (tile, 1), 0) + (step - micro * per_micro) * tile
    seg = t >> shift
    base = 1 + micros + 4 * micro
    limit = jnp.where(
        seg < 2,
        jnp.where(seg == 0, info[base], info[base + 1]),
        jnp.where(seg == 2, info[base + 2], info[base + 3]),
    )
    live = (t - (seg << shift)) < limit
    grad = jnp.where(live, cot[...].astype(F32), 0.0)
    d_2 = normal_back(grad * gain_2, n_2, s_2)
    dd = d_2.astype(LOW)
    d_down[...] = dd
    sums[0:1, :] += colsum(grad * n_2)
    sums[1:2, :] += colsum(grad)
    sums[2:3, :] += colsum(dd.astype(F32))
    d_hid = d_2
    for c in range(0, inner, part):
        g = mm(dd, wd[c : c + part, :], NT) * slope[:, c : c + part]
        g = g.astype(LOW)
        d_up[:, c : c + part] = g
        sum_up[:, c : c + part] += colsum(g.astype(F32))
        d_hid = d_hid + mm(g, wu[:, c : c + part], NT)
    d_1 = normal_back(d_hid * gain_1, n_1, s_1)
    d_res[...] = d_1
    da = d_1.astype(LOW)
    d_att[...] = da
    sums[3:4, :] += colsum(d_hid * n_1)
    sums[4:5, :] += colsum(d_hid)
    sums[5:6, :] += colsum(da.astype(F32))
    d_ctx[...] = mm(da, wo[...], NT).astype(LOW)


def middle_call(info, tokens, context, cotangent, vec, b_up, pieces, plan, micros, tile=256):
    rows, model = tokens.shape
    inner = b_up.shape[1]
    row = pl.BlockSpec((tile, model), lambda i, _: (i, 0))
    wide = pl.BlockSpec((tile, inner), lambda i, _: (i, 0))
    return pl.pallas_call(
        functools.partial(middle_kernel, plan, len(pieces), micros, rows // micros),
        out_shape=[
            shape((rows, model)),
            shape((rows, inner)),
            shape((rows, inner)),
            shape((rows, model)),
            shape((rows, model)),
            shape((rows, model), F32),
            shape((rows, model)),
            shape((rows, model)),
            shape((8, model), F32),
            shape((1, inner), F32),
        ],
        grid_spec=pltpu.PrefetchScalarGridSpec(
            num_scalar_prefetch=1,
            grid=(rows // tile,),
            in_specs=[row] * 3 + [whole(*vec.shape), whole(1, inner)] + [ANY] * len(pieces),
            out_specs=[row, wide, wide, row, row, row, row, row, whole(8, model), whole(1, inner)],
            scratch_shapes=[
                pltpu.VMEM((model, model), LOW),
                pltpu.VMEM((model, inner), LOW),
                pltpu.VMEM((inner, model), LOW),
                pltpu.VMEM((tile, inner), F32),
                pltpu.SemaphoreType.DMA((len(plan),)),
            ],
        ),
        compiler_params=params(1),
        cost_estimate=cost(
            8 * rows * model * inner + 4 * rows * model * model,
            20 * rows * model + 4 * rows * inner + 4 * model * inner,
            2 * rows * inner,
        ),
        name="middle",
    )(info, tokens, context, cotangent, vec, b_up, *pieces)


def attend_back_kernel(q, k, v, ctx, d_ctx, probs, grads, sums):
    keys, queries, values, d_c = k[...], q[...], v[...], d_ctx[...]
    k_t = keys.T
    d_t = d_c.T
    c_t = ctx[...].T
    lane = lax.broadcasted_iota(jnp.int32, keys.shape, 1)
    row = lax.broadcasted_iota(jnp.int32, d_t.shape, 0)
    spread = d_t.astype(F32) * c_t.astype(F32)
    d_q, d_k, d_v = [], [], []
    for h in range(2):
        part = slice(h * HEAD, (h + 1) * HEAD)
        delta = colsum(spread[part])
        mine = (row < HEAD) if h == 0 else (row >= HEAD)
        d_p = mm(values, jnp.where(mine, d_t, jnp.zeros_like(d_t)))
        p = probs[h]
        d_s = (p.astype(F32) * (d_p - delta)).astype(LOW)
        d_v.append(mm(p, d_c))
        d_k.append(mm(d_s, queries))
        d_q.append(mm(k_t[part], d_s))
    left = lane < HEAD
    dq = (jnp.concatenate(d_q, axis=0).T * 0.125).astype(LOW)
    dk = (jnp.where(left, d_k[0], d_k[1]) * 0.125).astype(LOW)
    dv = jnp.where(left, d_v[0], d_v[1]).astype(LOW)
    grads[0], grads[1], grads[2] = dq, dk, dv
    sums[0, 0:1, :] = colsum(dq.astype(F32))
    sums[0, 1:2, :] = colsum(dv.astype(F32))


def attend_back_call(q, k, v, context, d_context, probs, micros):
    rows, model = q.shape
    slots, pairs = rows // micros, model // 128
    pair = pl.BlockSpec((slots, 128), lambda i, j: (i, j))
    return pl.pallas_call(
        attend_back_kernel,
        out_shape=[shape((3, rows, model)), shape((micros, 8, model), F32)],
        grid=(micros, pairs),
        in_specs=[pair] * 5
        + [pl.BlockSpec((2, slots, slots), lambda i, j: (i * pairs + j, 0, 0))],
        out_specs=[
            pl.BlockSpec((3, slots, 128), lambda i, j: (0, i, j)),
            pl.BlockSpec((1, 8, 128), lambda i, j: (i, 0, j)),
        ],
        compiler_params=params(2),
        cost_estimate=cost(
            32 * rows * slots * model, 16 * rows * model + 4 * rows * slots * pairs
        ),
        name="attend_back",
    )(q, k, v, context, d_context, probs)


def wide_rows_kernel(info, left, right, *refs):
    acc = mm(left[...], right[...], TN)
    if len(refs) == 2:
        acc = acc + refs[0][0].astype(F32)
    refs[-1][0] = acc.astype(LOW)


def wide_rows_call(info, left, right, fsdp, core, got=None):
    rows, inner = left.shape
    model = right.shape[1]
    shard, chips = inner // fsdp, fsdp // 2
    block = pl.BlockSpec((1, shard, model), lambda j, _: (j, 0, 0))
    extra = [] if got is None else [got]
    return pl.pallas_call(
        wide_rows_kernel,
        out_shape=shape((chips, shard, model)),
        grid_spec=pltpu.PrefetchScalarGridSpec(
            num_scalar_prefetch=1,
            grid=(chips,),
            in_specs=[
                pl.BlockSpec((rows, shard), lambda j, info: (0, info[0] ^ (2 * j + core))),
                whole(rows, model),
            ]
            + [block] * len(extra),
            out_specs=block,
        ),
        compiler_params=params(1),
        cost_estimate=cost(rows * inner * model, rows * inner + 2 * rows * model + inner * model),
        name="grad_rows",
    )(info, left, right, *extra)


def shards_kernel(fsdp, info, left, right, away, home, acc):
    me = info[0]
    right = right[0] if len(right.shape) == 3 else right[...]
    acc[...] = mm(left[...], right, TN)
    shard = acc.shape[0] // fsdp
    for m in range(fsdp):
        at = pl.multiple_of((me ^ m) * shard, 16)
        target = away if m & 1 else home
        target[m >> 1] = acc[pl.ds(at, shard), :].astype(LOW)


def shards_call(info, left, right, fsdp, block=768):
    rows, model = left.shape
    shard, chips = model // fsdp, fsdp // 2
    if right.ndim == 3:
        n, stacked = right.shape[2], right.shape[0]
        grid = (stacked,)
        spec = pl.BlockSpec((1, rows, n), lambda i, _: (i, 0, 0))
        out = shape((chips, stacked * shard, n))
        out_spec = pl.BlockSpec((chips, shard, n), lambda i, _: (0, i, 0))
        block = n
    else:
        n, stacked = right.shape[1], 1
        grid = (n // block,)
        spec = pl.BlockSpec((rows, block), lambda i, _: (0, i))
        out = shape((chips, shard, n))
        out_spec = pl.BlockSpec((chips, shard, block), lambda i, _: (0, 0, i))
    return pl.pallas_call(
        functools.partial(shards_kernel, fsdp),
        out_shape=[out, out],
        grid_spec=pltpu.PrefetchScalarGridSpec(
            num_scalar_prefetch=1,
            grid=grid,
            in_specs=[whole(rows, model), spec],
            out_specs=[out_spec, out_spec],
            scratch_shapes=[pltpu.VMEM((model, block), F32)],
        ),
        compiler_params=params(1),
        cost_estimate=cost(
            2 * rows * model * n * stacked,
            2 * rows * model + 2 * rows * n * stacked + 2 * model * n * stacked,
        ),
        name="grad_shards",
    )(info, left, right)


def token_kernel(d_res, grads, wq, wk, wv, out):
    out[...] = (
        d_res[...]
        + mm(grads[0], wq[...], NT)
        + mm(grads[1], wk[...], NT)
        + mm(grads[2], wv[...], NT)
    )


def token_call(d_res, grads, wq, wk, wv, tile=256):
    rows, model = d_res.shape
    row = pl.BlockSpec((tile, model), lambda i: (i, 0))
    return pl.pallas_call(
        token_kernel,
        out_shape=shape((rows, model), F32),
        grid=(rows // tile,),
        in_specs=[row, pl.BlockSpec((3, tile, model), lambda i: (0, i, 0))]
        + [whole(model, model)] * 3,
        out_specs=row,
        compiler_params=params(1),
        cost_estimate=cost(6 * rows * model * model, 14 * rows * model + 6 * model * model),
        name="grad_tokens",
    )(d_res, grads, wq, wk, wv)


VECTORS = (1, 4, 6, 7, 8, 12, 13, 14, 10)


def on_device(sizes, tokens, cotangent, bucket, lengths, *shards):
    dp, fsdp = sizes
    me = lax.axis_index("fsdp").astype(jnp.int32)
    chip_bits = bits_of(fsdp)[1:]
    up, down = chip_bits + [1], chip_bits[::-1] + [1]
    rows, model = tokens.shape
    inner = shards[9].shape[1]
    shard, inner_shard = shards[0].shape[0], shards[11].shape[0]
    micros = bucket.shape[0]
    half = shard // 2
    aligned = shard % 32 == 0 and inner_shard % 128 == 0
    info = jnp.concatenate([me[None], bucket, lengths.reshape(-1)])

    vecs = jnp.concatenate([shards[i].reshape(-1, shard) for i in VECTORS], axis=0)
    first = jnp.concatenate([shards[0], shards[2][:half]], axis=0)
    second = jnp.concatenate([shards[3], shards[2][half:]], axis=0)
    got_v = gather_rel(vecs, down, fsdp)
    got_1, got_2 = gather_rel(first, up, fsdp), gather_rel(second, down, fsdp)
    got_o = gather_rel(shards[5], up, fsdp)
    got_up, got_down = gather_rel(shards[9], up, fsdp), gather_rel(shards[11], down, fsdp)
    n_vec = vecs.shape[0]
    all_vecs = reorder(jnp.stack(got_v), me).astype(F32)
    narrow = all_vecs[:, :8].transpose(1, 0, 2).reshape(8, model)
    b_up = all_vecs[:, 8:].reshape(1, inner)

    if aligned:
        n = fsdp
        qkv_pieces = got_1 + got_2
        qkv_plan = copy_plan(
            [
                (n, 0, 0, shard, 0, 0),
                (n, 0, shard, half, 1, 0),
                (n, n, shard, shard - half, 1, half),
                (n, n, 0, shard, 2, 0),
            ],
            shard,
        )
        mid_pieces = got_o + got_up + got_down
        mid_plan = copy_plan([(n, 0, 0, shard, 0, 0), (n, n, 0, shard, 1, 0)], shard)
        mid_plan += copy_plan([(n, 2 * n, 0, inner_shard, 2, 0)], inner_shard)
    else:
        w_k = [jnp.concatenate([a[shard:], b[shard:]], axis=0) for a, b in zip(got_1, got_2)]
        qkv_pieces = [
            place_rows([p[:shard] for p in got_1], me),
            place_rows(w_k, me),
            place_rows([p[:shard] for p in got_2], me),
        ]
        qkv_plan = [(i, 0, model, i, 0, 0, 0) for i in range(3)]
        mid_pieces = [place_rows(p, me) for p in (got_o, got_up, got_down)]
        mid_plan = [(i, 0, (model, model, inner)[i], i, 0, 0, 0) for i in range(3)]

    q, k, v, wq, wk, wv = qkv_call(info, tokens, narrow[:2], qkv_pieces, qkv_plan)
    context, probs = attend_call(info, q, k, v, micros)
    (output, active, d_up, hid_low, d_down, d_res, d_att, d_ctx, sums, sum_up) = middle_call(
        info, tokens, context, cotangent, narrow[2:], b_up, mid_pieces, mid_plan, micros
    )

    rs_up, rs_down = chip_bits, chip_bits[::-1]

    def finish(parts, order):
        mine = reduce_chips({2 * j: parts[j] for j in range(fsdp // 2)}, order, fsdp)
        return sum_over_dp(mine, dp).astype(F32)

    def both_cores(away, home, order):
        got = swap(away, 1, "fsdp", fsdp)
        return finish([add_low(home[j], got[j]) for j in range(fsdp // 2)], order)

    def relative(full):
        n = full.shape[0] // fsdp
        r = reorder(full.astype(LOW).reshape(fsdp, n, full.shape[1]), me)
        r = r.reshape(fsdp // 2, 2, n, full.shape[1])
        return r[:, 1], r[:, 0]

    finals = [None] * 15
    if aligned:
        away = wide_rows_call(info, active, d_down, fsdp, 1)
        got = swap(away, 1, "fsdp", fsdp)
        home = wide_rows_call(info, active, d_down, fsdp, 0, got)
        finals[11] = finish([home[j] for j in range(fsdp // 2)], rs_down)
        finals[9] = both_cores(*shards_call(info, hid_low, d_up, fsdp), rs_up)
        finals[5] = both_cores(*shards_call(info, context, d_att, fsdp), rs_up)
    else:
        finals[11] = both_cores(*relative(mm(active, d_down, TN)), rs_down)
        finals[9] = both_cores(*relative(mm(hid_low, d_up, TN)), rs_up)
        finals[5] = both_cores(*relative(mm(context, d_att, TN)), rs_up)
    grads, qv_sums = attend_back_call(q, k, v, context, d_ctx, probs, micros)
    if aligned:
        three = both_cores(*shards_call(info, tokens, grads, fsdp), rs_down)
    else:
        parts = [relative(mm(tokens, grads[i], TN)) for i in range(3)]
        away, home = (jnp.concatenate([p[i] for p in parts], axis=1) for i in range(2))
        three = both_cores(away, home, rs_down)
    finals[0], finals[2], finals[3] = three[:shard], three[shard : 2 * shard], three[2 * shard :]
    token_grads = token_call(d_res, grads, wq, wk, wv)

    qv = jnp.sum(qv_sums, axis=0)
    narrow_sums = jnp.stack(
        [qv[0], qv[1], sums[5], sums[3], sums[4], sums[2], sums[0], sums[1]]
    )
    by_shard = jnp.concatenate(
        [narrow_sums.reshape(8, fsdp, shard).transpose(1, 0, 2), sum_up.reshape(fsdp, -1, shard)],
        axis=1,
    )
    pad = (-n_vec) % (2 * dp)
    by_shard = jnp.pad(by_shard, ((0, 0), (0, pad), (0, 0)))
    small = both_cores(*relative(by_shard.reshape(fsdp * (n_vec + pad), shard)), rs_up)
    at = 0
    for i in VECTORS:
        n = shards[i].shape[0] // shard
        finals[i] = small[at : at + n].reshape(-1)
        at += n
    return (output, token_grads) + tuple(finals)


def solution(mesh):
    placed = (
        P(("dp", "fsdp"), None),
        P(("dp", "fsdp"), None),
        P(("dp", "fsdp")),
        P(("dp", "fsdp"), None),
        P("fsdp", None),
        P("fsdp"),
        P("fsdp", None),
        P("fsdp", None),
        P("fsdp"),
        P("fsdp", None),
        P("fsdp"),
        P("fsdp"),
        P("fsdp"),
        P("fsdp", None),
        P("fsdp"),
        P("fsdp", None),
        P("fsdp"),
        P("fsdp"),
        P("fsdp"),
    )
    sizes = (mesh.shape["dp"], mesh.shape["fsdp"])
    return jax.shard_map(
        functools.partial(on_device, sizes),
        mesh=mesh,
        in_specs=placed,
        out_specs=(
            P(("dp", "fsdp"), None),
            P(("dp", "fsdp"), None),
            P("fsdp", None),
            P("fsdp"),
            P("fsdp", None),
            P("fsdp", None),
            P("fsdp"),
            P("fsdp", None),
            P("fsdp"),
            P("fsdp"),
            P("fsdp"),
            P("fsdp", None),
            P("fsdp"),
            P("fsdp", None),
            P("fsdp"),
            P("fsdp"),
            P("fsdp"),
        ),
        check_vma=False,
    )
```
